32 devices in a mesh: row: 4 (over x, core), col: 8 (over z, y).
Axes of the slice: x: 2, y: 2, z: 4, core: 2. Of those that a mesh axis runs over, the one named last changes fastest.
Arguments:
- masters: float32 [128, 4096], P('col'), may hold values from -6 to 6
- inst_master: int32 [64, 128], P('row', 'col'), may hold values from 0 to 127
- inst_orient: int32 [64, 128], P('row', 'col'), may hold values from 0 to 3
- owner_map: int32 [128], replicated, may hold values from 0 to 127, each once
- tile_free: float32 [4096, 8192], P('row', 'col'), may hold values from -3 to 3
- target: float32 [4096, 8192], P('row', 'col'), may hold values from 0 to 1
- kernel_spectra: float32 [2, 128, 8, 128], replicated, may hold values from -6 to 6
- socs_weights: float32 [8], replicated, may hold values from 0.05 to 1
Outputs:
- resist: float32 [4096, 8192], P('row', 'col')
- new_mask: float32 [4096, 8192], P('row', 'col')
- masters_out: float32 [128, 4096], P('col')
The draws below stay inside these ranges and needn't reach their ends.
Inputs may be any that keep to these rules, and one draw needn't show every extreme that they name: `inst_orient`: bit 0 reverses a cell's rows, bit 1 its columns. `owner_map`: each storage row is used by exactly one master; storage row r lies on index r // 16 of col.
All inputs are finite; a program needn't handle non-finite values.
Results may differ from the reference program's by a relative error of at most 0.0092.
Values may be sent and summed in bfloat16 or wider, within the bound.
A program may use at most 128 MiB of HBM per device.

```python
import math
import jax
import jax.numpy as jnp
import numpy as np
from jax import lax

TILE = 512
TPD = 2
HALO = 64
CELL = 64
BAND = 128
NK = 8
ITERS = 1
PAD = 640
NM = 128
ROWS = 4096
COLS = 8192
GRID_R = 64
GRID_C = 128
N_ROW = 4
N_COL = 8


def place_ends(values, own_key, least, high):
    dims = values.shape
    spot = [jax.random.randint(jax.random.fold_in(own_key, axis), (), 0, dims[axis]) for axis in range(len(dims))]
    values = values.at[tuple(spot)].set(least)
    longest = dims.index(max(dims))
    spot[longest] = (spot[longest] + 1) % dims[longest]
    return values.at[tuple(spot)].set(high)


def block_scale(rng, extent, shards, low, largest):
    def one(position, shards_of):
        draws = jax.random.uniform(jax.random.fold_in(jax.random.fold_in(rng, 6), position), (shards_of,), jnp.float32, low / len(shards), largest / len(shards))
        return jnp.repeat(jnp.exp(draws), extent[position] // shards_of).reshape((-1,) + (1,) * (len(extent) - position - 1))

    gain = one(*shards[0])
    for cut in shards[1:]:
        gain = gain * one(*cut)
    return gain


def rank_bounds(count, skew):
    portions = [(1 << 20) // math.isqrt(standing ** skew) + 1 for standing in range(1, count + 1)]
    deviation = 1 + sum(portions) // (1 << 30)
    return np.cumsum(np.array([max(1, weight // deviation) for weight in portions]))


def ranked(own_key, shape, count, slope):
    listing = rank_bounds(count, slope)
    lot = jax.random.randint(jax.random.fold_in(own_key, 1), shape, 0, int(listing[count - 1]))
    standing = jnp.searchsorted(jnp.asarray(listing, jnp.int32), lot, side="right")
    return jax.random.permutation(jax.random.fold_in(own_key, 2), count)[standing].astype(jnp.int32)


def bell_draw(stream_key, extent, deviation, reach, shards=(), kind=jnp.bfloat16):
    gain = block_scale(stream_key, extent, shards, -0.22, 0.18) if shards else 1.0
    entries = jax.random.normal(stream_key, extent, jnp.float32) * deviation * gain
    return jnp.minimum(jnp.maximum(entries, -reach), reach).astype(kind)


def setup_inputs(seed: int = 0) -> dict:
    key_of = jax.random.split(jax.random.key(seed), 9)
    return {
        "masters": bell_draw(key_of[0], (NM, CELL * CELL), 1.0, 6.0, ((0, 8),), jnp.float32),
        "inst_master": place_ends(ranked(key_of[1], (GRID_R, GRID_C), NM, 2), jax.random.fold_in(key_of[1], 3), 0, NM - 1).astype(jnp.int32),
        "inst_orient": place_ends(jax.random.randint(key_of[2], (GRID_R, GRID_C), 0, 4), jax.random.fold_in(key_of[2], 1), 0, 3).astype(jnp.int32),
        "owner_map": jax.random.permutation(key_of[3], NM).astype(jnp.int32),
        "tile_free": bell_draw(key_of[4], (ROWS, COLS), 0.5, 3.0, ((0, 4), (1, 8)), jnp.float32),
        "target": jnp.clip(1.0 * jax.random.uniform(key_of[5], (ROWS, COLS), jnp.float32) ** block_scale(key_of[5], (ROWS, COLS), ((0, 4), (1, 8)), -0.2, 0.2), 0.0, 1.0),
        "kernel_spectra": bell_draw(key_of[6], (2, BAND, NK, BAND), 1.0, 6.0, (), jnp.float32),
        "socs_weights": jnp.clip(jnp.exp(jax.random.uniform(key_of[7], (NK,), jnp.float32, math.log(0.05), math.log(1.0))), 0.05, 1.0),
    }


step_free = 1.0
step_master = 0.05
resist_gain = 2.0
resist_level = 1.8


def dot_plain(left, right):
    return jnp.dot(left, right, preferred_element_type=jnp.float32)


def dot_right_t(left, right):
    return lax.dot_general(left, right, (((1,), (1,)), ((), ())), preferred_element_type=jnp.float32)


def dot_left_t(left, right):
    return lax.dot_general(left, right, (((0,), (0,)), ((), ())), preferred_element_type=jnp.float32)


def tables(pad_side, band_side):
    freqs = jnp.arange(band_side, dtype=jnp.int32) - band_side // 2
    pixels = jnp.arange(pad_side, dtype=jnp.int32)
    phases = (freqs[:, None] * pixels[None, :]) % pad_side
    angles = phases.astype(jnp.float32) * (2.0 * math.pi / pad_side)
    return jnp.cos(angles).astype(jnp.bfloat16), jnp.sin(angles).astype(jnp.bfloat16)


def tile_step(padded, target, spectra, weights, halo_side):
    pad_side = padded.shape[0]
    band_side = spectra.shape[1]
    kernels = spectra.shape[2]
    tile_side = pad_side - 2 * halo_side
    cos_full, sin_full = tables(pad_side, band_side)
    cos_in = cos_full[:, halo_side:halo_side + tile_side]
    sin_in = sin_full[:, halo_side:halo_side + tile_side]
    forw_re = dot_plain(cos_full, padded).astype(jnp.bfloat16)
    forw_im = (-dot_plain(sin_full, padded)).astype(jnp.bfloat16)
    spec_re = (dot_right_t(forw_re, cos_full) - dot_right_t(forw_im, sin_full)) / pad_side
    spec_im = (-dot_right_t(forw_re, sin_full) - dot_right_t(forw_im, cos_full)) / pad_side
    kern_re = spectra[0]
    kern_im = spectra[1]
    amp_re = (kern_re * spec_re[:, None, :] - kern_im * spec_im[:, None, :]).astype(jnp.bfloat16)
    amp_im = (kern_re * spec_im[:, None, :] + kern_im * spec_re[:, None, :]).astype(jnp.bfloat16)
    amp_re = amp_re.reshape(band_side, kernels * band_side)
    amp_im = amp_im.reshape(band_side, kernels * band_side)
    half_re = (dot_left_t(cos_in, amp_re) - dot_left_t(sin_in, amp_im)).astype(jnp.bfloat16)
    half_im = (dot_left_t(cos_in, amp_im) + dot_left_t(sin_in, amp_re)).astype(jnp.bfloat16)
    half_re = half_re.reshape(tile_side * kernels, band_side)
    half_im = half_im.reshape(tile_side * kernels, band_side)
    field_re = (dot_plain(half_re, cos_in) - dot_plain(half_im, sin_in)) / band_side
    field_im = (dot_plain(half_re, sin_in) + dot_plain(half_im, cos_in)) / band_side
    field_re = field_re.reshape(tile_side, kernels, tile_side)
    field_im = field_im.reshape(tile_side, kernels, tile_side)
    scaled = weights[None, :, None]
    intensity = jnp.sum(scaled * (field_re * field_re + field_im * field_im), axis=1)
    resist = jax.nn.sigmoid(resist_gain * (intensity - resist_level))
    slopes = 2.0 * (resist - target) * resist_gain * resist * (1.0 - resist)
    back_re = (2.0 / band_side * scaled * slopes[:, None, :] * field_re).astype(jnp.bfloat16)
    back_im = (2.0 / band_side * scaled * slopes[:, None, :] * field_im).astype(jnp.bfloat16)
    back_re = back_re.reshape(tile_side * kernels, tile_side)
    back_im = back_im.reshape(tile_side * kernels, tile_side)
    bhalf_re = (dot_right_t(back_re, cos_in) + dot_right_t(back_im, sin_in)).astype(jnp.bfloat16)
    bhalf_im = (dot_right_t(back_im, cos_in) - dot_right_t(back_re, sin_in)).astype(jnp.bfloat16)
    bhalf_re = bhalf_re.reshape(tile_side, kernels * band_side)
    bhalf_im = bhalf_im.reshape(tile_side, kernels * band_side)
    bamp_re = (dot_plain(cos_in, bhalf_re) + dot_plain(sin_in, bhalf_im)).reshape(band_side, kernels, band_side)
    bamp_im = (dot_plain(cos_in, bhalf_im) - dot_plain(sin_in, bhalf_re)).reshape(band_side, kernels, band_side)
    bspec_re = (jnp.sum(kern_re * bamp_re + kern_im * bamp_im, axis=1) / pad_side).astype(jnp.bfloat16)
    bspec_im = (jnp.sum(kern_re * bamp_im - kern_im * bamp_re, axis=1) / pad_side).astype(jnp.bfloat16)
    bforw_re = (dot_plain(bspec_re, cos_in) - dot_plain(bspec_im, sin_in)).astype(jnp.bfloat16)
    bforw_im = (-dot_plain(bspec_re, sin_in) - dot_plain(bspec_im, cos_in)).astype(jnp.bfloat16)
    gradient = dot_left_t(cos_in, bforw_re) - dot_left_t(sin_in, bforw_im)
    return resist, gradient


def orient_cells(cells, orient):
    flip_first = (orient % 2) == 1
    flip_second = (orient // 2) == 1
    cells = jnp.where(flip_first[..., None, None], cells[..., ::-1, :], cells)
    cells = jnp.where(flip_second[..., None, None], cells[..., :, ::-1], cells)
    return cells


def assemble(master_rows, slots, orient, cell_side):
    grid_rows, grid_cols = slots.shape
    cells = jnp.take(master_rows, slots.reshape(-1), axis=0)
    cells = cells.reshape(grid_rows, grid_cols, cell_side, cell_side)
    cells = orient_cells(cells, orient)
    return cells.transpose(0, 2, 1, 3).reshape(grid_rows * cell_side, grid_cols * cell_side)


def cells_of(image, orient, cell_side):
    grid_rows, grid_cols = orient.shape
    cells = image.reshape(grid_rows, cell_side, grid_cols, cell_side).transpose(0, 2, 1, 3)
    cells = orient_cells(cells, orient)
    return cells.reshape(grid_rows * grid_cols, cell_side * cell_side)


def smooth(master_rows, cell_side):
    grids = master_rows.reshape(-1, cell_side, cell_side)
    framed = jnp.pad(grids, ((0, 0), (1, 1), (1, 1)))
    beside_all = framed[:, 2:, 1:-1] + framed[:, :-2, 1:-1] + framed[:, 1:-1, 2:] + framed[:, 1:-1, :-2]
    return (0.5 * grids + 0.125 * beside_all).reshape(master_rows.shape)


def stitch(tiles, tile_rows, tile_cols):
    return tiles.reshape(tile_rows, tile_cols, TILE, TILE).transpose(0, 2, 1, 3).reshape(tile_rows * TILE, tile_cols * TILE)


def reference(masters, inst_master, inst_orient, owner_map, tile_free, target, kernel_spectra, socs_weights):
    slots = jnp.take(owner_map, inst_master)
    master_rows = masters
    free_field = tile_free
    resist = jnp.zeros_like(tile_free)
    tile_rows = N_ROW * TPD
    tile_cols = N_COL * TPD
    for sweep_index in range(ITERS):
        shading = jnp.tanh(assemble(master_rows, slots, inst_orient, CELL) + free_field)
        framed = jnp.pad(shading.astype(jnp.bfloat16), HALO)

        def one_tile(tile_index):
            row_at = tile_index // tile_cols
            col_at = tile_index % tile_cols
            window = lax.dynamic_slice(framed, (row_at * TILE, col_at * TILE), (PAD, PAD))
            goal_tile = lax.dynamic_slice(target, (row_at * TILE, col_at * TILE), (TILE, TILE))
            return tile_step(window, goal_tile, kernel_spectra, socs_weights, HALO)

        resist_tiles, grad_tiles = lax.map(one_tile, jnp.arange(tile_rows * tile_cols, dtype=jnp.int32))
        resist = stitch(resist_tiles, tile_rows, tile_cols)
        grad_param = stitch(grad_tiles, tile_rows, tile_cols) * (1.0 - shading * shading)
        free_field = free_field - step_free * grad_param
        cell_grads = cells_of(grad_param, inst_orient, CELL)
        master_grad = jax.ops.segment_sum(cell_grads, slots.reshape(-1), num_segments=NM)
        master_rows = smooth(master_rows - step_master * master_grad, CELL)
    new_mask = jnp.tanh(assemble(master_rows, slots, inst_orient, CELL) + free_field)
    return resist, new_mask, master_rows
```

```python
import functools
import math

import jax
import jax.numpy as jnp
import numpy as np
from jax import lax
from jax.experimental import pallas as pl
from jax.experimental.pallas import tpu as pltpu
from jax.sharding import PartitionSpec as P

TILE = 512
TPD = 2
HALO = 64
CELL = 64
LANES = 128
HALF = CELL // 2

step_free = 1.0
step_master = 0.05
resist_gain = 2.0
resist_level = 1.8


def dot(left, right):
    return jnp.dot(left, right, preferred_element_type=jnp.float32)


def tables(pad_side, band_side, halo, tile):
    freqs = np.arange(band_side, dtype=np.int64) - band_side // 2
    phases = (freqs[:, None] * np.arange(pad_side)[None, :]) % pad_side
    angles = phases.astype(np.float32) * np.float32(2.0 * math.pi / pad_side)
    cos = np.cos(angles)
    sin = np.sin(angles)
    cos_in = cos[:, halo : halo + tile]
    sin_in = sin[:, halo : halo + tile]
    cs_full = np.concatenate([cos, sin], 0)
    cs_in = np.concatenate([cos_in, sin_in], 0)
    field = np.block([[cos_in, sin_in], [-sin_in, cos_in]])
    parts = (cs_full, cs_full.T, cs_in, cs_in.T, field, field.T)
    return [jnp.asarray(np.ascontiguousarray(p).astype(jnp.bfloat16)) for p in parts]


def placements():
    rows_place = np.zeros((4, CELL, 2 * CELL), np.float32)
    cols_place = np.zeros((4, LANES, LANES), np.float32)
    for f in range(4):
        for side in range(2):
            flip = (f >> side) & 1
            for r in range(HALF):
                for h in range(2):
                    y = 2 * r + h
                    rows_place[f, CELL - 1 - y if flip else y, side * CELL + h * HALF + r] = 1
            for x in range(CELL):
                cols_place[f, side * CELL + x, side * CELL + (CELL - 1 - x if flip else x)] = 1
    cast = lambda v: jnp.asarray(np.ascontiguousarray(v).astype(jnp.bfloat16))
    return cast(rows_place), cast(rows_place.transpose(0, 2, 1)), cast(cols_place)


def left_mask(rows):
    return lax.broadcasted_iota(jnp.int32, (rows, LANES), 1) < CELL


def pair_codes(inst_ref, orient_ref, owner_ref, a, b):
    s0 = owner_ref[inst_ref[a, b]]
    s1 = owner_ref[inst_ref[a, b + 1]]
    o0 = orient_ref[a, b]
    o1 = orient_ref[a, b + 1]
    return s0, s1, (o0 & 1) + 2 * (o1 & 1), (o0 >> 1) + 2 * (o1 >> 1)


def assemble_pair(table_ref, rows_ref, cols_ref, codes):
    s0, s1, fr, fc = codes
    left = left_mask(HALF)
    p0 = table_ref[s0].astype(jnp.float32)
    p1 = table_ref[s1].astype(jnp.float32)
    q0 = pltpu.roll(p0, CELL, 1)
    q1 = pltpu.roll(p1, CELL, 1)
    parts = [
        jnp.where(left, p0, 0.0),
        jnp.where(left, q0, 0.0),
        jnp.where(left, 0.0, q1),
        jnp.where(left, 0.0, p1),
    ]
    split = jnp.concatenate(parts, axis=0).astype(jnp.bfloat16)
    placed = dot(rows_ref[fr], split).astype(jnp.bfloat16)
    return dot(placed, cols_ref[fc])


def image_kernel(emit_mask, inst_ref, orient_ref, owner_ref, table_ref, free_ref, rows_ref, cols_ref, *outs):
    a = pl.program_id(0)
    for pair in range(free_ref.shape[1] // LANES):
        codes = pair_codes(inst_ref, orient_ref, owner_ref, a, 2 * pair)
        cells = assemble_pair(table_ref, rows_ref, cols_ref, codes)
        lanes = slice(pair * LANES, (pair + 1) * LANES)
        value = jnp.tanh(cells + free_ref[:, lanes])
        outs[0][:, lanes] = value
        if emit_mask:
            outs[1][:, lanes] = value.astype(jnp.bfloat16)


def whole_spec(array):
    zeros = (0,) * array.ndim
    return pl.BlockSpec(array.shape, lambda *_: zeros)


def image(inst, orient, owner, table, free, rows_place, cols_place, emit_mask):
    height, width = free.shape
    strip = pl.BlockSpec((CELL, width), lambda a, *_: (a, 0))
    out_shape = [jax.ShapeDtypeStruct(free.shape, jnp.float32)]
    if emit_mask:
        out_shape.append(jax.ShapeDtypeStruct(free.shape, jnp.bfloat16))
    return pl.pallas_call(
        functools.partial(image_kernel, emit_mask),
        grid_spec=pltpu.PrefetchScalarGridSpec(
            num_scalar_prefetch=3,
            grid=(height // CELL,),
            in_specs=[whole_spec(table), strip, whole_spec(rows_place), whole_spec(cols_place)],
            out_specs=[strip] * len(out_shape),
        ),
        out_shape=out_shape,
        name="image",
    )(inst, orient, owner, table, free, rows_place, cols_place)


def tile_kernel(
    inst_ref, orient_ref, owner_ref, weights_ref,
    padded_ref, target_ref, shading_ref, free_ref, spectra_ref,
    cs_full_ref, cs_full_t_ref, cs_in_ref, cs_in_t_ref, field_ref, field_t_ref,
    rows_t_ref, cols_ref,
    resist_ref, new_free_ref, sums_ref,
    amp_s, half_s, bhalf_s, field_s, grad_s, sums_s,
):
    i = pl.program_id(0)
    j = pl.program_id(1)
    band = spectra_ref.shape[1]
    kernels = spectra_ref.shape[2]
    tile = target_ref.shape[0]
    pad_side = cs_full_ref.shape[1]
    block = field_s.shape[1]
    wide = 2 * band

    @pl.when((i == 0) & (j == 0))
    def _():
        sums_s[...] = jnp.zeros_like(sums_s)

    window = padded_ref[
        pl.ds(pl.multiple_of(i * tile, 128), pad_side), pl.ds(pl.multiple_of(j * tile, 128), pad_side)
    ]
    forw = dot(cs_full_ref[...], window).astype(jnp.bfloat16)
    spec = dot(forw, cs_full_t_ref[...])
    spec_re = (spec[:band, :band] + spec[band:, band:]) / pad_side
    spec_im = (spec[band:, :band] - spec[:band, band:]) / pad_side
    for k in range(kernels):
        kern_re = spectra_ref[0, :, k, :]
        kern_im = spectra_ref[1, :, k, :]
        amp_re = (kern_re * spec_re - kern_im * spec_im).astype(jnp.bfloat16)
        amp_im = (kern_re * spec_im + kern_im * spec_re).astype(jnp.bfloat16)
        at = k * wide
        amp_s[:band, at : at + band] = amp_re
        amp_s[band:, at : at + band] = -amp_im
        amp_s[:band, at + band : at + wide] = amp_im
        amp_s[band:, at + band : at + wide] = amp_re
    for k in range(kernels):
        cols = slice(k * wide, (k + 1) * wide)
        half_s[:, cols] = dot(cs_in_t_ref[...], amp_s[:, cols]).astype(jnp.bfloat16)

    def rows_step(n, carry):
        rows = pl.ds(pl.multiple_of(n * block, block), block)
        intensity = jnp.zeros((block, tile), jnp.float32)
        for k in range(kernels):
            field = dot(half_s[rows, k * wide : (k + 1) * wide], field_ref[...])
            field_s[k] = field
            re = field[:, :tile]
            im = field[:, tile:]
            intensity += (weights_ref[k] / (band * band)) * (re * re + im * im)
        resist = jax.nn.sigmoid(resist_gain * (intensity - resist_level))
        resist_ref[rows, :] = resist
        slopes = 2.0 * (resist - target_ref[rows, :]) * resist_gain * resist * (1.0 - resist)
        for k in range(kernels):
            scale = slopes * (2.0 * weights_ref[k] / (band * band))
            re = (field_s[k, :, :tile] * scale).astype(jnp.bfloat16)
            im = (field_s[k, :, tile:] * scale).astype(jnp.bfloat16)
            back = jnp.concatenate([re, im], axis=1)
            bhalf_s[rows, k * wide : (k + 1) * wide] = dot(back, field_t_ref[...]).astype(jnp.bfloat16)
        return carry

    lax.fori_loop(0, tile // block, rows_step, 0)
    bspec_re = jnp.zeros((band, band), jnp.float32)
    bspec_im = jnp.zeros((band, band), jnp.float32)
    for k in range(kernels):
        bamp = dot(cs_in_ref[...], bhalf_s[:, k * wide : (k + 1) * wide])
        bamp_re = bamp[:band, :band] + bamp[band:, band:]
        bamp_im = bamp[:band, band:] - bamp[band:, :band]
        kern_re = spectra_ref[0, :, k, :]
        kern_im = spectra_ref[1, :, k, :]
        bspec_re += kern_re * bamp_re + kern_im * bamp_im
        bspec_im += kern_re * bamp_im - kern_im * bamp_re
    bspec = jnp.concatenate([bspec_re / pad_side, bspec_im / pad_side], axis=1).astype(jnp.bfloat16)
    bforw = dot(bspec, field_ref[...]).astype(jnp.bfloat16)
    bforw = jnp.concatenate([bforw[:, :tile], bforw[:, tile:]], axis=0)
    gradient = dot(cs_in_t_ref[...], bforw)
    shading = shading_ref[...]
    grad_param = gradient * (1.0 - shading * shading)
    new_free_ref[...] = free_ref[...] - step_free * grad_param
    grad_s[...] = grad_param.astype(jnp.bfloat16)
    cells = tile // CELL
    left = left_mask(HALF)

    def cells_step(a, carry):
        rows = pl.ds(pl.multiple_of(a * CELL, CELL), CELL)
        for pair in range(cells // 2):
            s0, s1, fr, fc = pair_codes(
                inst_ref, orient_ref, owner_ref, i * cells + a, j * cells + 2 * pair
            )
            piece = grad_s[rows, pair * LANES : (pair + 1) * LANES]
            turned = dot(piece, cols_ref[fc]).astype(jnp.bfloat16)
            split = dot(rows_t_ref[fr], turned)
            a0 = split[:HALF]
            a1 = pltpu.roll(split[HALF : 2 * HALF], CELL, 1)
            b0 = pltpu.roll(split[2 * HALF : 3 * HALF], CELL, 1)
            b1 = split[3 * HALF :]
            sums_s[s0] += jnp.where(left, a0, a1)
            sums_s[s1] += jnp.where(left, b0, b1)
        return carry

    lax.fori_loop(0, cells, cells_step, 0)

    @pl.when((i == pl.num_programs(0) - 1) & (j == pl.num_programs(1) - 1))
    def _():
        sums_ref[...] = sums_s[...].astype(jnp.bfloat16)


def tile_steps(inst, orient, owner, weights, padded, target, shading, free, spectra, consts, rows_t, cols_place, masters):
    height, width = target.shape
    band = spectra.shape[1]
    kernels = spectra.shape[2]
    block = 64
    tile_spec = pl.BlockSpec((TILE, TILE), lambda i, j, *_: (i, j))
    sums_shape = (masters, HALF, LANES)
    once = [padded, None, None, None, spectra, *consts, rows_t, cols_place]
    return pl.pallas_call(
        tile_kernel,
        grid_spec=pltpu.PrefetchScalarGridSpec(
            num_scalar_prefetch=4,
            grid=(height // TILE, width // TILE),
            in_specs=[tile_spec if v is None else whole_spec(v) for v in once],
            out_specs=[tile_spec, tile_spec, pl.BlockSpec(sums_shape, lambda *_: (0, 0, 0))],
            scratch_shapes=[
                pltpu.VMEM((2 * band, kernels * 2 * band), jnp.bfloat16),
                pltpu.VMEM((TILE, kernels * 2 * band), jnp.bfloat16),
                pltpu.VMEM((TILE, kernels * 2 * band), jnp.bfloat16),
                pltpu.VMEM((kernels, block, 2 * TILE), jnp.float32),
                pltpu.VMEM((TILE, TILE), jnp.bfloat16),
                pltpu.VMEM(sums_shape, jnp.float32),
            ],
        ),
        out_shape=[
            jax.ShapeDtypeStruct(target.shape, jnp.float32),
            jax.ShapeDtypeStruct(target.shape, jnp.float32),
            jax.ShapeDtypeStruct(sums_shape, jnp.bfloat16),
        ],
        compiler_params=pltpu.CompilerParams(vmem_limit_bytes=60 * 1024 * 1024),
        name="tile_steps",
    )(inst, orient, owner, weights, padded, target, shading, free, spectra, *consts, rows_t, cols_place)


def smooth_packed(cells):
    lane = lax.broadcasted_iota(jnp.int32, cells.shape, cells.ndim - 1)
    x = lane % CELL
    before = jnp.where(x == 0, 0.0, jnp.roll(cells, 1, axis=-1))
    after = jnp.where(x == CELL - 1, 0.0, jnp.roll(cells, -1, axis=-1))
    other = jnp.roll(cells, CELL, axis=-1)
    edge = jnp.zeros_like(other[:, :1])
    up = jnp.concatenate([edge, other[:, :-1]], axis=1)
    down = jnp.concatenate([other[:, 1:], edge], axis=1)
    beside = before + after + other + jnp.where(lane < CELL, up, down)
    return 0.5 * cells + 0.125 * beside


def padded_2(value, sides, width):
    for axis, dim in sides:
        peers, length = (lax.axis_size(axis), value.shape[dim])
        up = [(i, (i + 1) % peers) for i in range(peers - 1)]
        down = [(j, i) for i, j in up]
        last = lax.slice_in_dim(value, length - width, length, axis=dim)
        initial = lax.slice_in_dim(value, 0, width, axis=dim)
        before = lax.ppermute(last, axis, up)
        after = lax.ppermute(initial, axis, down)
        value = jnp.concatenate([before, value, after], axis=dim)
    return value


def per_device(
    masters, inst_master, inst_orient, owner_map, tile_free, target, kernel_spectra, socs_weights
):
    stored = masters.shape[0]
    total = owner_map.shape[0]
    consts = tables(TILE + 2 * HALO, kernel_spectra.shape[1], HALO, TILE)
    rows_place, rows_t, cols_place = placements()
    own = masters.reshape(stored, HALF, LANES)
    table = lax.all_gather(own.astype(jnp.bfloat16), "col", axis=0, tiled=True)
    shading, mask = image(
        inst_master, inst_orient, owner_map, table, tile_free, rows_place, cols_place, True
    )
    padded = padded_2(mask, (("row", 0), ("col", 1)), HALO)
    resist, new_free, sums = tile_steps(
        inst_master, inst_orient, owner_map, socs_weights, padded, target, shading, tile_free,
        kernel_spectra, consts, rows_t, cols_place, total,
    )
    part = lax.psum_scatter(sums, "col", scatter_dimension=0, tiled=True)
    summed = lax.psum(part, "row").astype(jnp.float32)
    fresh = smooth_packed(own - step_master * summed).astype(jnp.bfloat16)
    table = lax.all_gather(fresh, "col", axis=0, tiled=True)
    (new_mask,) = image(
        inst_master, inst_orient, owner_map, table, new_free, rows_place, cols_place, False
    )
    return (resist, new_mask, fresh.astype(jnp.float32).reshape(masters.shape))


def solution(mesh):
    in_specs = (
        P("col", None),
        P("row", "col"),
        P("row", "col"),
        P(),
        P("row", "col"),
        P("row", "col"),
        P(),
        P(),
    )
    out_specs = (P("row", "col"), P("row", "col"), P("col", None))
    return jax.shard_map(
        per_device, mesh=mesh, in_specs=in_specs, out_specs=out_specs, check_vma=False
    )
```

```python
import functools
import math

import jax
import jax.numpy as jnp
import numpy as np
from jax import lax
from jax.experimental import pallas as pl
from jax.experimental.pallas import tpu as pltpu
from jax.sharding import PartitionSpec as P

TILE = 512
TPD = 2
HALO = 64
CELL = 64
LANES = 128
HALF = CELL // 2
BLOCK = 256

step_free = 1.0
step_master = 0.05
resist_gain = 2.0
resist_level = 1.8


def dot(left, right):
    return jnp.dot(left, right, preferred_element_type=jnp.float32)


def tables(pad_side, band_side, halo, tile):
    freqs = np.arange(band_side, dtype=np.int64) - band_side // 2
    phases = (freqs[:, None] * np.arange(pad_side)[None, :]) % pad_side
    angles = phases.astype(np.float32) * np.float32(2.0 * math.pi / pad_side)
    cos = np.cos(angles)
    sin = np.sin(angles)
    cos_in = cos[:, halo : halo + tile]
    sin_in = sin[:, halo : halo + tile]
    cs_full = np.concatenate([cos, sin], 0)
    cs_lanes = np.pad(cs_full, ((0, 0), (LANES - halo, LANES - halo)))
    cs_in = np.concatenate([cos_in, sin_in], 0)
    field = np.block([[cos_in, sin_in], [-sin_in, cos_in]])
    parts = (cs_full, cs_lanes.T, cs_in, cs_in.T, field, field.T)
    return [jnp.asarray(np.ascontiguousarray(p).astype(jnp.bfloat16)) for p in parts]


def placements():
    rows_place = np.zeros((4, CELL, 2 * CELL), np.float32)
    cols_place = np.zeros((4, LANES, LANES), np.float32)
    for f in range(4):
        for side in range(2):
            flip = (f >> side) & 1
            for r in range(HALF):
                for h in range(2):
                    y = 2 * r + h
                    rows_place[f, CELL - 1 - y if flip else y, side * CELL + h * HALF + r] = 1
            for x in range(CELL):
                cols_place[f, side * CELL + x, side * CELL + (CELL - 1 - x if flip else x)] = 1
    cast = lambda v: jnp.asarray(np.ascontiguousarray(v).astype(jnp.bfloat16))
    return cast(rows_place), cast(rows_place.transpose(0, 2, 1)), cast(cols_place)


def left_mask(rows):
    return lax.broadcasted_iota(jnp.int32, (rows, LANES), 1) < CELL


def pair_codes(inst_ref, orient_ref, owner_ref, a, b):
    s0 = owner_ref[inst_ref[a, b]]
    s1 = owner_ref[inst_ref[a, b + 1]]
    o0 = orient_ref[a, b]
    o1 = orient_ref[a, b + 1]
    return s0, s1, (o0 & 1) + 2 * (o1 & 1), (o0 >> 1) + 2 * (o1 >> 1)


def assemble_pair(table_ref, rows_ref, cols_ref, codes):
    s0, s1, fr, fc = codes
    left = left_mask(HALF)
    p0 = table_ref[s0].astype(jnp.float32)
    p1 = table_ref[s1].astype(jnp.float32)
    q0 = pltpu.roll(p0, CELL, 1)
    q1 = pltpu.roll(p1, CELL, 1)
    parts = [
        jnp.where(left, p0, 0.0),
        jnp.where(left, q0, 0.0),
        jnp.where(left, 0.0, q1),
        jnp.where(left, 0.0, p1),
    ]
    split = jnp.concatenate(parts, axis=0).astype(jnp.bfloat16)
    placed = dot(rows_ref[fr], split).astype(jnp.bfloat16)
    return dot(placed, cols_ref[fc])


def image_kernel(emit_mask, inst_ref, orient_ref, owner_ref, table_ref, free_ref, rows_ref, cols_ref, *outs):
    a = pl.program_id(0)
    for pair in range(free_ref.shape[1] // LANES):
        codes = pair_codes(inst_ref, orient_ref, owner_ref, a, 2 * pair)
        cells = assemble_pair(table_ref, rows_ref, cols_ref, codes)
        lanes = slice(pair * LANES, (pair + 1) * LANES)
        value = jnp.tanh(cells + free_ref[:, lanes])
        outs[0][:, lanes] = value
        if emit_mask:
            outs[1][:, lanes] = value.astype(jnp.bfloat16)


def whole_spec(array):
    zeros = (0,) * array.ndim
    return pl.BlockSpec(array.shape, lambda *_: zeros)


def image(inst, orient, owner, table, free, rows_place, cols_place, emit_mask):
    height, width = free.shape
    strip = pl.BlockSpec((CELL, width), lambda a, *_: (a, 0))
    out_shape = [jax.ShapeDtypeStruct(free.shape, jnp.float32)]
    if emit_mask:
        out_shape.append(jax.ShapeDtypeStruct(free.shape, jnp.bfloat16))
    return pl.pallas_call(
        functools.partial(image_kernel, emit_mask),
        grid_spec=pltpu.PrefetchScalarGridSpec(
            num_scalar_prefetch=3,
            grid=(height // CELL,),
            in_specs=[whole_spec(table), strip, whole_spec(rows_place), whole_spec(cols_place)],
            out_specs=[strip] * len(out_shape),
        ),
        out_shape=out_shape,
        name="image",
    )(inst, orient, owner, table, free, rows_place, cols_place)


def tile_kernel(
    inst_ref, orient_ref, owner_ref, weights_ref,
    padded_ref, target_ref, shading_ref, free_ref, spectra_ref,
    cs_full_ref, cs_full_t_ref, cs_in_ref, cs_in_t_ref, field_ref, field_t_ref,
    rows_t_ref, cols_ref,
    resist_ref, new_free_ref, sums_ref,
    amp_s, half_s, bhalf_s, field_s, grad_s, sums_s,
):
    i = pl.program_id(0)
    j = pl.program_id(1)
    band = spectra_ref.shape[1]
    kernels = spectra_ref.shape[2]
    tile = target_ref.shape[0]
    pad_side = cs_full_ref.shape[1]
    pad_lanes = cs_full_t_ref.shape[0]
    block = field_s.shape[1]
    wide = 2 * band

    @pl.when((i == 0) & (j == 0))
    def _():
        sums_s[...] = jnp.zeros_like(sums_s)

    window = padded_ref[
        pl.ds(pl.multiple_of(i * tile, 128), pad_side), pl.ds(pl.multiple_of(j * tile, 128), pad_lanes)
    ]
    forw = dot(cs_full_ref[...], window).astype(jnp.bfloat16)
    spec = dot(forw, cs_full_t_ref[...])
    spec_re = (spec[:band, :band] + spec[band:, band:]) / pad_side
    spec_im = (spec[band:, :band] - spec[:band, band:]) / pad_side
    for k in range(kernels):
        kern_re = spectra_ref[0, :, k, :]
        kern_im = spectra_ref[1, :, k, :]
        amp_re = (kern_re * spec_re - kern_im * spec_im).astype(jnp.bfloat16)
        amp_im = (kern_re * spec_im + kern_im * spec_re).astype(jnp.bfloat16)
        at = k * wide
        amp_s[:band, at : at + band] = amp_re
        amp_s[band:, at : at + band] = -amp_im
        amp_s[:band, at + band : at + wide] = amp_im
        amp_s[band:, at + band : at + wide] = amp_re
    for k in range(kernels):
        cols = slice(k * wide, (k + 1) * wide)
        half_s[:, cols] = dot(cs_in_t_ref[...], amp_s[:, cols]).astype(jnp.bfloat16)

    def rows_step(n, carry):
        rows = pl.ds(pl.multiple_of(n * block, block), block)
        intensity = jnp.zeros((block, tile), jnp.float32)
        for k in range(kernels):
            field = dot(half_s[rows, k * wide : (k + 1) * wide], field_ref[...])
            field_s[k] = field
            re = field[:, :tile]
            im = field[:, tile:]
            intensity += (weights_ref[k] / (band * band)) * (re * re + im * im)
        resist = jax.nn.sigmoid(resist_gain * (intensity - resist_level))
        resist_ref[rows, :] = resist
        slopes = 2.0 * (resist - target_ref[rows, :]) * resist_gain * resist * (1.0 - resist)
        for k in range(kernels):
            scale = slopes * (2.0 * weights_ref[k] / (band * band))
            re = (field_s[k, :, :tile] * scale).astype(jnp.bfloat16)
            im = (field_s[k, :, tile:] * scale).astype(jnp.bfloat16)
            back = jnp.concatenate([re, im], axis=1)
            bhalf_s[rows, k * wide : (k + 1) * wide] = dot(back, field_t_ref[...]).astype(jnp.bfloat16)
        return carry

    lax.fori_loop(0, tile // block, rows_step, 0)
    bspec_re = jnp.zeros((band, band), jnp.float32)
    bspec_im = jnp.zeros((band, band), jnp.float32)
    for k in range(kernels):
        bamp = dot(cs_in_ref[...], bhalf_s[:, k * wide : (k + 1) * wide])
        bamp_re = bamp[:band, :band] + bamp[band:, band:]
        bamp_im = bamp[:band, band:] - bamp[band:, :band]
        kern_re = spectra_ref[0, :, k, :]
        kern_im = spectra_ref[1, :, k, :]
        bspec_re += kern_re * bamp_re + kern_im * bamp_im
        bspec_im += kern_re * bamp_im - kern_im * bamp_re
    bspec = jnp.concatenate([bspec_re / pad_side, bspec_im / pad_side], axis=1).astype(jnp.bfloat16)
    bforw = dot(bspec, field_ref[...]).astype(jnp.bfloat16)
    bforw = jnp.concatenate([bforw[:, :tile], bforw[:, tile:]], axis=0)
    gradient = dot(cs_in_t_ref[...], bforw)
    shading = shading_ref[...]
    grad_param = gradient * (1.0 - shading * shading)
    new_free_ref[...] = free_ref[...] - step_free * grad_param
    grad_s[...] = grad_param.astype(jnp.bfloat16)
    cells = tile // CELL
    left = left_mask(HALF)

    def cells_step(a, carry):
        rows = pl.ds(pl.multiple_of(a * CELL, CELL), CELL)
        for pair in range(cells // 2):
            s0, s1, fr, fc = pair_codes(
                inst_ref, orient_ref, owner_ref, i * cells + a, j * cells + 2 * pair
            )
            piece = grad_s[rows, pair * LANES : (pair + 1) * LANES]
            turned = dot(piece, cols_ref[fc]).astype(jnp.bfloat16)
            split = dot(rows_t_ref[fr], turned)
            a0 = split[:HALF]
            a1 = pltpu.roll(split[HALF : 2 * HALF], CELL, 1)
            b0 = pltpu.roll(split[2 * HALF : 3 * HALF], CELL, 1)
            b1 = split[3 * HALF :]
            sums_s[s0] += jnp.where(left, a0, a1)
            sums_s[s1] += jnp.where(left, b0, b1)
        return carry

    lax.fori_loop(0, cells, cells_step, 0)

    @pl.when((i == pl.num_programs(0) - 1) & (j == pl.num_programs(1) - 1))
    def _():
        sums_ref[...] = sums_s[...].astype(jnp.bfloat16)


def tile_steps(inst, orient, owner, weights, padded, target, shading, free, spectra, consts, rows_t, cols_place, masters):
    height, width = target.shape
    band = spectra.shape[1]
    kernels = spectra.shape[2]
    block = BLOCK
    tile_spec = pl.BlockSpec((TILE, TILE), lambda i, j, *_: (i, j))
    sums_shape = (masters, HALF, LANES)
    once = [padded, None, None, None, spectra, *consts, rows_t, cols_place]
    return pl.pallas_call(
        tile_kernel,
        grid_spec=pltpu.PrefetchScalarGridSpec(
            num_scalar_prefetch=4,
            grid=(height // TILE, width // TILE),
            in_specs=[tile_spec if v is None else whole_spec(v) for v in once],
            out_specs=[tile_spec, tile_spec, pl.BlockSpec(sums_shape, lambda *_: (0, 0, 0))],
            scratch_shapes=[
                pltpu.VMEM((2 * band, kernels * 2 * band), jnp.bfloat16),
                pltpu.VMEM((TILE, kernels * 2 * band), jnp.bfloat16),
                pltpu.VMEM((TILE, kernels * 2 * band), jnp.bfloat16),
                pltpu.VMEM((kernels, block, 2 * TILE), jnp.float32),
                pltpu.VMEM((TILE, TILE), jnp.bfloat16),
                pltpu.VMEM(sums_shape, jnp.float32),
            ],
        ),
        out_shape=[
            jax.ShapeDtypeStruct(target.shape, jnp.float32),
            jax.ShapeDtypeStruct(target.shape, jnp.float32),
            jax.ShapeDtypeStruct(sums_shape, jnp.bfloat16),
        ],
        compiler_params=pltpu.CompilerParams(vmem_limit_bytes=60 * 1024 * 1024),
        name="tile_steps",
    )(inst, orient, owner, weights, padded, target, shading, free, spectra, *consts, rows_t, cols_place)


MESH = pl.DeviceIdType.MESH
VM = pl.BlockSpec(memory_space=pltpu.VMEM)


def split_id(flat, n_col):
    return (lax.div(flat, n_col), lax.rem(flat, n_col))


def greet(peers):
    barrier = pltpu.get_barrier_semaphore()
    for peer in peers:
        pl.semaphore_signal(barrier, inc=1, device_id=peer, device_id_type=MESH)
    pl.semaphore_wait(barrier, len(peers))


def gather_kernel(n_col, own_ref, table_ref, send_sem, recv_sem):
    r = lax.axis_index("row")
    c = lax.axis_index("col")
    stored = own_ref.shape[0]
    greet([(r, lax.rem(c + t, n_col)) for t in range(1, n_col)])
    here = table_ref.at[pl.ds(c * stored, stored)]
    copies = [
        pltpu.make_async_remote_copy(
            src_ref=own_ref,
            dst_ref=here,
            send_sem=send_sem.at[t],
            recv_sem=recv_sem.at[t],
            device_id=(r, lax.rem(c + t, n_col)),
            device_id_type=MESH,
        )
        for t in range(1, n_col)
    ]
    for copy in copies:
        copy.start()
    table_ref[pl.ds(c * stored, stored)] = own_ref[...]
    for copy in copies:
        copy.wait()


def gather_masters(own, n_col):
    return pl.pallas_call(
        functools.partial(gather_kernel, n_col),
        in_specs=[VM],
        out_specs=VM,
        out_shape=jax.ShapeDtypeStruct((n_col * own.shape[0],) + own.shape[1:], own.dtype),
        scratch_shapes=[pltpu.SemaphoreType.DMA((n_col,)), pltpu.SemaphoreType.DMA((n_col,))],
        compiler_params=pltpu.CompilerParams(collective_id=0, has_side_effects=True),
        name="gather_masters",
    )(own)


def halo_kernel(n_row, n_col, mask_ref, out_ref, send_sem, recv_sem):
    r = lax.axis_index("row")
    c = lax.axis_index("col")
    height, width = mask_ref.shape
    row_parts = {
        -1: (slice(0, HALO), slice(HALO + height, 2 * HALO + height)),
        0: (slice(0, height), slice(HALO, HALO + height)),
        1: (slice(height - HALO, height), slice(0, HALO)),
    }
    col_parts = {
        -1: (slice(0, LANES), slice(LANES + width, 2 * LANES + width)),
        0: (slice(0, width), slice(LANES, LANES + width)),
        1: (slice(width - LANES, width), slice(0, LANES)),
    }
    moves = [(0, 1), (0, -1), (1, 0), (-1, 0), (1, 1), (1, -1), (-1, 1), (-1, -1)]
    ids = [(lax.rem(r + n_row + dr, n_row), lax.rem(c + n_col + dc, n_col)) for dr, dc in moves]
    greet(ids)
    copies = []
    for at, (dr, dc) in enumerate(moves):
        src_rows, dst_rows = row_parts[dr]
        src_cols, dst_cols = col_parts[dc]
        copy = pltpu.make_async_remote_copy(
            src_ref=mask_ref.at[src_rows, src_cols],
            dst_ref=out_ref.at[dst_rows, dst_cols],
            send_sem=send_sem.at[at],
            recv_sem=recv_sem.at[at],
            device_id=ids[at],
            device_id_type=MESH,
        )
        copy.start()
        copies.append(copy)
    out_ref[HALO : HALO + height, LANES : LANES + width] = mask_ref[...]
    for copy in copies:
        copy.wait()

    @pl.when(r == 0)
    def _():
        out_ref[:HALO, :] = jnp.zeros((HALO, width + 2 * LANES), out_ref.dtype)

    @pl.when(r == n_row - 1)
    def _():
        out_ref[HALO + height :, :] = jnp.zeros((HALO, width + 2 * LANES), out_ref.dtype)

    @pl.when(c == 0)
    def _():
        out_ref[:, :LANES] = jnp.zeros((height + 2 * HALO, LANES), out_ref.dtype)

    @pl.when(c == n_col - 1)
    def _():
        out_ref[:, LANES + width :] = jnp.zeros((height + 2 * HALO, LANES), out_ref.dtype)


def with_halo(mask, n_row, n_col):
    height, width = mask.shape
    return pl.pallas_call(
        functools.partial(halo_kernel, n_row, n_col),
        in_specs=[VM],
        out_specs=VM,
        out_shape=jax.ShapeDtypeStruct((height + 2 * HALO, width + 2 * LANES), mask.dtype),
        scratch_shapes=[pltpu.SemaphoreType.DMA((8,)), pltpu.SemaphoreType.DMA((8,))],
        compiler_params=pltpu.CompilerParams(collective_id=1, has_side_effects=True),
        name="with_halo",
    )(mask)


def smooth_packed(cells):
    count = cells.shape[0]
    flat = cells.reshape(count * HALF, LANES)
    lane = lax.broadcasted_iota(jnp.int32, flat.shape, 1)
    x = lane % CELL
    row = lax.broadcasted_iota(jnp.int32, flat.shape, 0) % HALF
    before = jnp.where(x == 0, 0.0, pltpu.roll(flat, 1, 1))
    after = jnp.where(x == CELL - 1, 0.0, pltpu.roll(flat, LANES - 1, 1))
    other = pltpu.roll(flat, CELL, 1)
    up = jnp.where(row == 0, 0.0, pltpu.roll(other, 1, 0))
    down = jnp.where(row == HALF - 1, 0.0, pltpu.roll(other, count * HALF - 1, 0))
    beside = before + after + other + jnp.where(lane < CELL, up, down)
    return (0.5 * flat + 0.125 * beside).reshape(cells.shape)


def update_kernel(
    n_row, n_col, sums_ref, own_ref, table_ref,
    parts, fresh, send_sem, recv_sem, send2_sem, recv2_sem,
):
    r = lax.axis_index("row")
    c = lax.axis_index("col")
    count = n_row * n_col
    me = r * n_col + c
    stored = own_ref.shape[0]
    share = stored // n_row
    barrier = pltpu.get_barrier_semaphore()

    def first_row(flat):
        pr, pc = split_id(flat, n_col)
        return pc * stored + pr * share

    def hello(t, carry):
        pl.semaphore_signal(
            barrier, inc=1, device_id=split_id(lax.rem(me + t, count), n_col), device_id_type=MESH
        )
        return carry

    lax.fori_loop(1, count, hello, 0)
    pl.semaphore_wait(barrier, count - 1)

    def part_copy(t):
        peer = lax.rem(me + t, count)
        return pltpu.make_async_remote_copy(
            src_ref=sums_ref.at[pl.ds(first_row(peer), share)],
            dst_ref=parts.at[t],
            send_sem=send_sem.at[t],
            recv_sem=recv_sem.at[t],
            device_id=split_id(peer, n_col),
            device_id_type=MESH,
        )

    def start_part(t, carry):
        part_copy(t).start()
        return carry

    lax.fori_loop(1, count, start_part, 0)

    def add_part(t, total):
        part_copy(t).wait_recv()
        return total + parts[t].astype(jnp.float32)

    mine = first_row(me)
    total = lax.fori_loop(1, count, add_part, sums_ref[pl.ds(mine, share)].astype(jnp.float32))
    updated = own_ref[pl.ds(r * share, share)] - step_master * total
    value = smooth_packed(updated).astype(jnp.bfloat16)
    fresh[...] = value
    table_ref[pl.ds(mine, share)] = value

    def end_part(t, carry):
        part_copy(t).wait_send()
        return carry

    lax.fori_loop(1, count, end_part, 0)

    def fresh_copy(t):
        return pltpu.make_async_remote_copy(
            src_ref=fresh,
            dst_ref=table_ref.at[pl.ds(mine, share)],
            send_sem=send2_sem.at[t],
            recv_sem=recv2_sem.at[t],
            device_id=split_id(lax.rem(me + t, count), n_col),
            device_id_type=MESH,
        )

    def start_fresh(t, carry):
        fresh_copy(t).start()
        return carry

    def end_fresh(t, carry):
        fresh_copy(t).wait()
        return carry

    lax.fori_loop(1, count, start_fresh, 0)
    lax.fori_loop(1, count, end_fresh, 0)


def update_masters(sums, own, n_row, n_col):
    count = n_row * n_col
    piece = (own.shape[0] // n_row,) + own.shape[1:]
    return pl.pallas_call(
        functools.partial(update_kernel, n_row, n_col),
        in_specs=[VM, VM],
        out_specs=VM,
        out_shape=jax.ShapeDtypeStruct(sums.shape, jnp.bfloat16),
        scratch_shapes=[
            pltpu.VMEM((count,) + piece, jnp.bfloat16),
            pltpu.VMEM(piece, jnp.bfloat16),
            pltpu.SemaphoreType.DMA((count,)),
            pltpu.SemaphoreType.DMA((count,)),
            pltpu.SemaphoreType.DMA((count,)),
            pltpu.SemaphoreType.DMA((count,)),
        ],
        compiler_params=pltpu.CompilerParams(collective_id=2, has_side_effects=True),
        name="update_masters",
    )(sums, own)


def per_device(
    masters, inst_master, inst_orient, owner_map, tile_free, target, kernel_spectra, socs_weights
):
    stored = masters.shape[0]
    total = owner_map.shape[0]
    consts = tables(TILE + 2 * HALO, kernel_spectra.shape[1], HALO, TILE)
    rows_place, rows_t, cols_place = placements()
    own = masters.reshape(stored, HALF, LANES)
    n_row = lax.axis_size("row")
    n_col = lax.axis_size("col")
    table = gather_masters(own.astype(jnp.bfloat16), n_col)
    shading, mask = image(
        inst_master, inst_orient, owner_map, table, tile_free, rows_place, cols_place, True
    )
    padded = with_halo(mask, n_row, n_col)
    resist, new_free, sums = tile_steps(
        inst_master, inst_orient, owner_map, socs_weights, padded, target, shading, tile_free,
        kernel_spectra, consts, rows_t, cols_place, total,
    )
    table = update_masters(sums, own, n_row, n_col)
    fresh = lax.dynamic_slice_in_dim(table, lax.axis_index("col") * stored, stored, 0)
    (new_mask,) = image(
        inst_master, inst_orient, owner_map, table, new_free, rows_place, cols_place, False
    )
    return (resist, new_mask, fresh.astype(jnp.float32).reshape(masters.shape))


def solution(mesh):
    in_specs = (
        P("col", None),
        P("row", "col"),
        P("row", "col"),
        P(),
        P("row", "col"),
        P("row", "col"),
        P(),
        P(),
    )
    out_specs = (P("row", "col"), P("row", "col"), P("col", None))
    return jax.shard_map(
        per_device, mesh=mesh, in_specs=in_specs, out_specs=out_specs, check_vma=False
    )
```

```python
import functools
import math

import jax
import jax.numpy as jnp
import numpy as np
from jax import lax
from jax.experimental import pallas as pl
from jax.experimental.pallas import tpu as pltpu
from jax.sharding import PartitionSpec as P

TILE = 512
TPD = 2
HALO = 64
CELL = 64
LANES = 128
HALF = CELL // 2
BLOCK = 512

step_free = 1.0
step_master = 0.05
resist_gain = 2.0
resist_level = 1.8


def dot(left, right):
    return jnp.dot(left, right, preferred_element_type=jnp.float32)


def tables(pad_side, band_side, halo, tile):
    freqs = np.arange(band_side, dtype=np.int64) - band_side // 2
    phases = (freqs[:, None] * np.arange(pad_side)[None, :]) % pad_side
    angles = phases.astype(np.float32) * np.float32(2.0 * math.pi / pad_side)
    cos = np.cos(angles)
    sin = np.sin(angles)
    cos_in = cos[:, halo : halo + tile]
    sin_in = sin[:, halo : halo + tile]
    cs_full = np.concatenate([cos, sin], 0)
    cs_lanes = np.pad(cs_full, ((0, 0), (LANES - halo, LANES - halo)))
    cs_in = np.concatenate([cos_in, sin_in], 0)
    field = np.block([[cos_in, sin_in], [-sin_in, cos_in]])
    parts = (cs_full, cs_lanes.T, cs_in, cs_in.T, field, field.T)
    return [jnp.asarray(np.ascontiguousarray(p).astype(jnp.bfloat16)) for p in parts]


def placements():
    rows_place = np.zeros((4, CELL, 2 * CELL), np.float32)
    cols_place = np.zeros((4, LANES, LANES), np.float32)
    for f in range(4):
        for side in range(2):
            flip = (f >> side) & 1
            for r in range(HALF):
                for h in range(2):
                    y = 2 * r + h
                    rows_place[f, CELL - 1 - y if flip else y, side * CELL + h * HALF + r] = 1
            for x in range(CELL):
                cols_place[f, side * CELL + x, side * CELL + (CELL - 1 - x if flip else x)] = 1
    cast = lambda v: jnp.asarray(np.ascontiguousarray(v).astype(jnp.bfloat16))
    return cast(rows_place), cast(rows_place.transpose(0, 2, 1)), cast(cols_place)


def left_mask(rows):
    return lax.broadcasted_iota(jnp.int32, (rows, LANES), 1) < CELL


def pair_codes(inst_ref, orient_ref, owner_ref, a, b):
    s0 = owner_ref[inst_ref[a, b]]
    s1 = owner_ref[inst_ref[a, b + 1]]
    o0 = orient_ref[a, b]
    o1 = orient_ref[a, b + 1]
    return s0, s1, (o0 & 1) + 2 * (o1 & 1), (o0 >> 1) + 2 * (o1 >> 1)


def assemble_pair(table_ref, rows_ref, cols_ref, codes):
    s0, s1, fr, fc = codes
    left = left_mask(HALF)
    p0 = table_ref[s0].astype(jnp.float32)
    p1 = table_ref[s1].astype(jnp.float32)
    q0 = pltpu.roll(p0, CELL, 1)
    q1 = pltpu.roll(p1, CELL, 1)
    parts = [
        jnp.where(left, p0, 0.0),
        jnp.where(left, q0, 0.0),
        jnp.where(left, 0.0, q1),
        jnp.where(left, 0.0, p1),
    ]
    split = jnp.concatenate(parts, axis=0).astype(jnp.bfloat16)
    placed = dot(rows_ref[fr], split).astype(jnp.bfloat16)
    return dot(placed, cols_ref[fc])


def image_kernel(emit_mask, inst_ref, orient_ref, owner_ref, table_ref, free_ref, rows_ref, cols_ref, *outs):
    a = pl.program_id(0)
    for pair in range(free_ref.shape[1] // LANES):
        codes = pair_codes(inst_ref, orient_ref, owner_ref, a, 2 * pair)
        cells = assemble_pair(table_ref, rows_ref, cols_ref, codes)
        lanes = slice(pair * LANES, (pair + 1) * LANES)
        value = jnp.tanh(cells + free_ref[:, lanes])
        outs[0][:, lanes] = value
        if emit_mask:
            outs[1][:, lanes] = value.astype(jnp.bfloat16)
            left = left_mask(HALF)
            if pair == 0:
                turned = pltpu.roll(value[HALF:], CELL, 1)
                outs[2][...] = jnp.where(left, value[:HALF], turned).astype(jnp.bfloat16)
            if pair == free_ref.shape[1] // LANES - 1:
                turned = pltpu.roll(value[:HALF], CELL, 1)
                outs[3][...] = jnp.where(left, turned, value[HALF:]).astype(jnp.bfloat16)


def whole_spec(array):
    zeros = (0,) * array.ndim
    return pl.BlockSpec(array.shape, lambda *_: zeros)


def image(inst, orient, owner, table, free, rows_place, cols_place, emit_mask):
    height, width = free.shape
    strip = pl.BlockSpec((CELL, width), lambda a, *_: (a, 0))
    out_shape = [jax.ShapeDtypeStruct(free.shape, jnp.float32)]
    out_specs = [strip]
    if emit_mask:
        edge = jax.ShapeDtypeStruct((height // 2, LANES), jnp.bfloat16)
        edge_spec = pl.BlockSpec((HALF, LANES), lambda a, *_: (a, 0))
        out_shape += [jax.ShapeDtypeStruct(free.shape, jnp.bfloat16), edge, edge]
        out_specs += [strip, edge_spec, edge_spec]
    return pl.pallas_call(
        functools.partial(image_kernel, emit_mask),
        grid_spec=pltpu.PrefetchScalarGridSpec(
            num_scalar_prefetch=3,
            grid=(height // CELL,),
            in_specs=[whole_spec(table), strip, whole_spec(rows_place), whole_spec(cols_place)],
            out_specs=out_specs,
        ),
        out_shape=out_shape,
        name="image",
    )(inst, orient, owner, table, free, rows_place, cols_place)


def tile_kernel(
    inst_ref, orient_ref, owner_ref, weights_ref,
    padded_ref, target_ref, shading_ref, free_ref, spectra_ref,
    cs_full_ref, cs_full_t_ref, cs_in_ref, cs_in_t_ref, field_ref, field_t_ref,
    rows_t_ref, cols_ref,
    resist_ref, new_free_ref, sums_ref,
    amp_s, half_s, bhalf_s, field_s, grad_s, sums_s,
):
    i = pl.program_id(0)
    j = pl.program_id(1)
    band = spectra_ref.shape[1]
    kernels = spectra_ref.shape[2]
    tile = target_ref.shape[0]
    pad_side = cs_full_ref.shape[1]
    pad_lanes = cs_full_t_ref.shape[0]
    block = field_s.shape[1]
    wide = 2 * band

    @pl.when((i == 0) & (j == 0))
    def _():
        sums_s[...] = jnp.zeros_like(sums_s)

    window = padded_ref[
        pl.ds(pl.multiple_of(i * tile, 128), pad_side), pl.ds(pl.multiple_of(j * tile, 128), pad_lanes)
    ]
    forw = dot(cs_full_ref[...], window).astype(jnp.bfloat16)
    spec = dot(forw, cs_full_t_ref[...])
    spec_re = (spec[:band, :band] + spec[band:, band:]) / pad_side
    spec_im = (spec[band:, :band] - spec[:band, band:]) / pad_side
    for k in range(kernels):
        kern_re = spectra_ref[0, :, k, :]
        kern_im = spectra_ref[1, :, k, :]
        amp_re = (kern_re * spec_re - kern_im * spec_im).astype(jnp.bfloat16)
        amp_im = (kern_re * spec_im + kern_im * spec_re).astype(jnp.bfloat16)
        at = k * wide
        amp_s[:band, at : at + band] = amp_re
        amp_s[band:, at : at + band] = -amp_im
        amp_s[:band, at + band : at + wide] = amp_im
        amp_s[band:, at + band : at + wide] = amp_re
    for k in range(kernels):
        cols = slice(k * wide, (k + 1) * wide)
        half_s[:, cols] = dot(cs_in_t_ref[...], amp_s[:, cols]).astype(jnp.bfloat16)

    def rows_step(n, carry):
        rows = pl.ds(pl.multiple_of(n * block, block), block)
        intensity = jnp.zeros((block, tile), jnp.float32)
        for k in range(kernels):
            field = dot(half_s[rows, k * wide : (k + 1) * wide], field_ref[...])
            field_s[k] = field
            re = field[:, :tile]
            im = field[:, tile:]
            intensity += (weights_ref[k] / (band * band)) * (re * re + im * im)
        resist = jax.nn.sigmoid(resist_gain * (intensity - resist_level))
        resist_ref[rows, :] = resist
        slopes = 2.0 * (resist - target_ref[rows, :]) * resist_gain * resist * (1.0 - resist)
        for k in range(kernels):
            scale = slopes * (2.0 * weights_ref[k] / (band * band))
            re = (field_s[k, :, :tile] * scale).astype(jnp.bfloat16)
            im = (field_s[k, :, tile:] * scale).astype(jnp.bfloat16)
            back = jnp.concatenate([re, im], axis=1)
            bhalf_s[rows, k * wide : (k + 1) * wide] = dot(back, field_t_ref[...]).astype(jnp.bfloat16)
        return carry

    lax.fori_loop(0, tile // block, rows_step, 0)
    bspec_re = jnp.zeros((band, band), jnp.float32)
    bspec_im = jnp.zeros((band, band), jnp.float32)
    for k in range(kernels):
        bamp = dot(cs_in_ref[...], bhalf_s[:, k * wide : (k + 1) * wide])
        bamp_re = bamp[:band, :band] + bamp[band:, band:]
        bamp_im = bamp[:band, band:] - bamp[band:, :band]
        kern_re = spectra_ref[0, :, k, :]
        kern_im = spectra_ref[1, :, k, :]
        bspec_re += kern_re * bamp_re + kern_im * bamp_im
        bspec_im += kern_re * bamp_im - kern_im * bamp_re
    bspec = jnp.concatenate([bspec_re / pad_side, bspec_im / pad_side], axis=1).astype(jnp.bfloat16)
    bforw = dot(bspec, field_ref[...]).astype(jnp.bfloat16)
    bforw = jnp.concatenate([bforw[:, :tile], bforw[:, tile:]], axis=0)
    gradient = dot(cs_in_t_ref[...], bforw)
    shading = shading_ref[...]
    grad_param = gradient * (1.0 - shading * shading)
    new_free_ref[...] = free_ref[...] - step_free * grad_param
    grad_s[...] = grad_param.astype(jnp.bfloat16)
    cells = tile // CELL
    left = left_mask(HALF)

    def cells_step(a, carry):
        rows = pl.ds(pl.multiple_of(a * CELL, CELL), CELL)
        for pair in range(cells // 2):
            s0, s1, fr, fc = pair_codes(
                inst_ref, orient_ref, owner_ref, i * cells + a, j * cells + 2 * pair
            )
            piece = grad_s[rows, pair * LANES : (pair + 1) * LANES]
            turned = dot(piece, cols_ref[fc]).astype(jnp.bfloat16)
            split = dot(rows_t_ref[fr], turned)
            a0 = split[:HALF]
            a1 = pltpu.roll(split[HALF : 2 * HALF], CELL, 1)
            b0 = pltpu.roll(split[2 * HALF : 3 * HALF], CELL, 1)
            b1 = split[3 * HALF :]
            sums_s[s0] += jnp.where(left, a0, a1)
            sums_s[s1] += jnp.where(left, b0, b1)
        return carry

    lax.fori_loop(0, cells, cells_step, 0)

    @pl.when((i == pl.num_programs(0) - 1) & (j == pl.num_programs(1) - 1))
    def _():
        sums_ref[...] = sums_s[...].astype(jnp.bfloat16)


def tile_steps(inst, orient, owner, weights, padded, target, shading, free, spectra, consts, rows_t, cols_place, masters):
    height, width = target.shape
    band = spectra.shape[1]
    kernels = spectra.shape[2]
    block = BLOCK
    tile_spec = pl.BlockSpec((TILE, TILE), lambda i, j, *_: (i, j))
    sums_shape = (masters, HALF, LANES)
    once = [padded, None, None, None, spectra, *consts, rows_t, cols_place]
    return pl.pallas_call(
        tile_kernel,
        grid_spec=pltpu.PrefetchScalarGridSpec(
            num_scalar_prefetch=4,
            grid=(height // TILE, width // TILE),
            in_specs=[tile_spec if v is None else whole_spec(v) for v in once],
            out_specs=[tile_spec, tile_spec, pl.BlockSpec(sums_shape, lambda *_: (0, 0, 0))],
            scratch_shapes=[
                pltpu.VMEM((2 * band, kernels * 2 * band), jnp.bfloat16),
                pltpu.VMEM((TILE, kernels * 2 * band), jnp.bfloat16),
                pltpu.VMEM((TILE, kernels * 2 * band), jnp.bfloat16),
                pltpu.VMEM((kernels, block, 2 * TILE), jnp.float32),
                pltpu.VMEM((TILE, TILE), jnp.bfloat16),
                pltpu.VMEM(sums_shape, jnp.float32),
            ],
        ),
        out_shape=[
            jax.ShapeDtypeStruct(target.shape, jnp.float32),
            jax.ShapeDtypeStruct(target.shape, jnp.float32),
            jax.ShapeDtypeStruct(sums_shape, jnp.bfloat16),
        ],
        compiler_params=pltpu.CompilerParams(vmem_limit_bytes=60 * 1024 * 1024),
        name="tile_steps",
    )(inst, orient, owner, weights, padded, target, shading, free, spectra, *consts, rows_t, cols_place)


MESH = pl.DeviceIdType.MESH
VM = pl.BlockSpec(memory_space=pltpu.VMEM)


def split_id(flat, n_col):
    return (lax.div(flat, n_col), lax.rem(flat, n_col))


def greet(peers):
    barrier = pltpu.get_barrier_semaphore()
    for peer in peers:
        pl.semaphore_signal(barrier, inc=1, device_id=peer, device_id_type=MESH)
    pl.semaphore_wait(barrier, len(peers))


def level_peers(n_row, n_col):
    r = lax.axis_index("row")
    c = lax.axis_index("col")
    long = n_col // 2
    z, y = lax.div(c, 2), lax.rem(c, 2)
    x, core = lax.div(r, 2), lax.rem(r, 2)
    p = x * 2 + y

    def z_at(t):
        return lax.rem(z + t + long, long)

    def p_at(t):
        q = lax.rem(p + t + n_row, n_row)
        return lax.div(q, 2), lax.rem(q, 2)

    return r, c, z, y, x, core, long, z_at, p_at


def gather_ids(n_row, n_col):
    r, c, z, y, x, core, long, z_at, p_at = level_peers(n_row, n_col)
    ids = [(r, z_at(t) * 2 + y) for t in range(1, long)]
    for t in range(1, n_row):
        px, py = p_at(t)
        ids.append((px * 2 + core, z * 2 + py))
    return ids + [(x * 2 + 1 - core, c)]


def gather_levels(n_row, n_col, own, table_ref, stored, send_sem, recv_sem):
    r, c, z, y, x, core, long, z_at, p_at = level_peers(n_row, n_col)
    share = stored // n_row

    def block(row, col):
        return table_ref.at[pl.ds(col * stored + row * share, share)]

    def make(src, dst, level, at, peer):
        return pltpu.make_async_remote_copy(
            src_ref=src,
            dst_ref=dst,
            send_sem=send_sem.at[level, at],
            recv_sem=recv_sem.at[level, at],
            device_id=peer,
            device_id_type=MESH,
        )

    partner = (x * 2 + 1 - core, c)
    mine = block(r, c)
    first = [make(own, mine, 0, t, (r, z_at(t) * 2 + y)) for t in range(1, long)]
    for copy in first:
        copy.start()
    second = []
    third = []
    for t in range(long):
        if t > 0:
            first[t - 1].wait_recv()
        here = block(r, z_at(-t) * 2 + y)
        src = own if t == 0 else here
        for q in range(1, n_row):
            px, py = p_at(q)
            copy = make(src, here, 1, t * n_row + q, (px * 2 + core, z * 2 + py))
            copy.start()
            second.append(copy)
        copy = make(src, here, 2, t * n_row, partner)
        copy.start()
        third.append(copy)
    for t in range(long):
        for q in range(1, n_row):
            second[t * (n_row - 1) + q - 1].wait_recv()
            px, py = p_at(-q)
            here = block(px * 2 + core, z_at(-t) * 2 + py)
            copy = make(here, here, 2, t * n_row + q, partner)
            copy.start()
            third.append(copy)
    for copy in third:
        copy.wait_recv()
    for copy in first + second + third:
        copy.wait_send()


def gather_sems(n_row, n_col):
    shape = (3, n_row * n_col // 2)
    return [pltpu.SemaphoreType.DMA(shape), pltpu.SemaphoreType.DMA(shape)]


def gather_kernel(n_row, n_col, own_ref, table_ref, send_sem, recv_sem):
    r = lax.axis_index("row")
    c = lax.axis_index("col")
    stored = own_ref.shape[0]
    share = stored // n_row
    greet(gather_ids(n_row, n_col))
    own = own_ref.at[pl.ds(r * share, share)]
    table_ref[pl.ds(c * stored + r * share, share)] = own_ref[pl.ds(r * share, share)]
    gather_levels(n_row, n_col, own, table_ref, stored, send_sem, recv_sem)


def gather_masters(own, n_row, n_col):
    return pl.pallas_call(
        functools.partial(gather_kernel, n_row, n_col),
        in_specs=[VM],
        out_specs=VM,
        out_shape=jax.ShapeDtypeStruct((n_col * own.shape[0],) + own.shape[1:], own.dtype),
        scratch_shapes=gather_sems(n_row, n_col),
        compiler_params=pltpu.CompilerParams(collective_id=0, has_side_effects=True),
        name="gather_masters",
    )(own)


def halo_kernel(
    n_row, n_col, mask_ref, edge_l_ref, edge_r_ref, out_ref, from_l, from_r, send_sem, recv_sem
):
    r = lax.axis_index("row")
    c = lax.axis_index("col")
    height, width = mask_ref.shape
    packed = height // 2
    middle = slice(LANES, LANES + width)
    row_parts = {
        -1: (slice(0, HALO), slice(HALO + height, 2 * HALO + height)),
        1: (slice(height - HALO, height), slice(0, HALO)),
    }
    edge_parts = {
        -1: (slice(0, HALF), slice(HALF + packed, 2 * HALF + packed)),
        0: (slice(0, packed), slice(HALF, HALF + packed)),
        1: (slice(packed - HALF, packed), slice(0, HALF)),
    }
    moves = [(0, 1), (0, -1), (1, 0), (-1, 0), (1, 1), (1, -1), (-1, 1), (-1, -1)]
    ids = [(lax.rem(r + n_row + dr, n_row), lax.rem(c + n_col + dc, n_col)) for dr, dc in moves]

    def inside(dr, dc):
        return (r + dr >= 0) & (r + dr < n_row) & (c + dc >= 0) & (c + dc < n_col)

    work = []
    for at, (dr, dc) in enumerate(moves):
        if dc == 0:
            src, dst = row_parts[dr]
            src, dst = mask_ref.at[src], out_ref.at[dst, middle]
        else:
            src, dst = edge_parts[dr]
            src = (edge_r_ref if dc == 1 else edge_l_ref).at[src]
            dst = (from_l if dc == 1 else from_r).at[dst]
        copy = pltpu.make_async_remote_copy(
            src_ref=src,
            dst_ref=dst,
            send_sem=send_sem.at[at],
            recv_sem=recv_sem.at[at],
            device_id=ids[at],
            device_id_type=MESH,
        )
        work.append((copy, dst, inside(dr, dc), inside(-dr, -dc)))
    greet(ids)
    for copy, dst, sends, gets in work:
        pl.when(sends)(copy.start)
    for copy, dst, sends, gets in work:

        @pl.when(jnp.logical_not(gets))
        def _():
            dst[...] = jnp.zeros(dst.shape, dst.dtype)

    out_ref[HALO : HALO + height, middle] = mask_ref[...]
    for copy, dst, sends, gets in work:
        pl.when(gets)(copy.wait_recv)
    left = left_mask(HALF)

    def unpack(a, carry):
        rows = pl.ds(pl.multiple_of(a * HALF, HALF), HALF)
        upper = pl.ds(pl.multiple_of(a * CELL, CELL), HALF)
        lower = pl.ds(pl.multiple_of(a * CELL + HALF, HALF), HALF)
        one = from_l[rows].astype(jnp.float32)
        two = from_r[rows].astype(jnp.float32)
        cast = lambda v: v.astype(jnp.bfloat16)
        last = slice(LANES + width, 2 * LANES + width)
        out_ref[upper, :LANES] = cast(jnp.where(left, 0.0, pltpu.roll(one, CELL, 1)))
        out_ref[lower, :LANES] = cast(jnp.where(left, 0.0, one))
        out_ref[upper, last] = cast(jnp.where(left, two, 0.0))
        out_ref[lower, last] = cast(jnp.where(left, pltpu.roll(two, CELL, 1), 0.0))
        return carry

    lax.fori_loop(0, (height + 2 * HALO) // CELL, unpack, 0)
    for copy, dst, sends, gets in work:
        pl.when(sends)(copy.wait_send)


def with_halo(mask, edge_l, edge_r, n_row, n_col):
    height, width = mask.shape
    return pl.pallas_call(
        functools.partial(halo_kernel, n_row, n_col),
        in_specs=[VM, VM, VM],
        out_specs=VM,
        out_shape=jax.ShapeDtypeStruct((height + 2 * HALO, width + 2 * LANES), mask.dtype),
        scratch_shapes=[
            pltpu.VMEM((height // 2 + 2 * HALF, LANES), mask.dtype),
            pltpu.VMEM((height // 2 + 2 * HALF, LANES), mask.dtype),
            pltpu.SemaphoreType.DMA((8,)),
            pltpu.SemaphoreType.DMA((8,)),
        ],
        compiler_params=pltpu.CompilerParams(collective_id=1, has_side_effects=True),
        name="with_halo",
    )(mask, edge_l, edge_r)


def smooth_packed(cells):
    count = cells.shape[0]
    flat = cells.reshape(count * HALF, LANES)
    lane = lax.broadcasted_iota(jnp.int32, flat.shape, 1)
    x = lane % CELL
    row = lax.broadcasted_iota(jnp.int32, flat.shape, 0) % HALF
    before = jnp.where(x == 0, 0.0, pltpu.roll(flat, 1, 1))
    after = jnp.where(x == CELL - 1, 0.0, pltpu.roll(flat, LANES - 1, 1))
    other = pltpu.roll(flat, CELL, 1)
    up = jnp.where(row == 0, 0.0, pltpu.roll(other, 1, 0))
    down = jnp.where(row == HALF - 1, 0.0, pltpu.roll(other, count * HALF - 1, 0))
    beside = before + after + other + jnp.where(lane < CELL, up, down)
    return (0.5 * flat + 0.125 * beside).reshape(cells.shape)


def update_kernel(
    n_row, n_col, sums_ref, own_ref, table_ref,
    parts, fresh, send_sem, recv_sem, send2_sem, recv2_sem,
):
    r = lax.axis_index("row")
    c = lax.axis_index("col")
    count = n_row * n_col
    me = r * n_col + c
    stored = own_ref.shape[0]
    share = stored // n_row
    barrier = pltpu.get_barrier_semaphore()

    def first_row(flat):
        pr, pc = split_id(flat, n_col)
        return pc * stored + pr * share

    def hello(t, carry):
        pl.semaphore_signal(
            barrier, inc=1, device_id=split_id(lax.rem(me + t, count), n_col), device_id_type=MESH
        )
        return carry

    lax.fori_loop(1, count, hello, 0)
    pl.semaphore_wait(barrier, count - 1)

    def part_copy(t):
        peer = lax.rem(me + t, count)
        return pltpu.make_async_remote_copy(
            src_ref=sums_ref.at[pl.ds(first_row(peer), share)],
            dst_ref=parts.at[t],
            send_sem=send_sem.at[t],
            recv_sem=recv_sem.at[t],
            device_id=split_id(peer, n_col),
            device_id_type=MESH,
        )

    def start_part(t, carry):
        part_copy(t).start()
        return carry

    lax.fori_loop(1, count, start_part, 0)

    def add_part(t, total):
        part_copy(t).wait_recv()
        return total + parts[t].astype(jnp.float32)

    mine = first_row(me)
    total = lax.fori_loop(1, count, add_part, sums_ref[pl.ds(mine, share)].astype(jnp.float32))
    updated = own_ref[pl.ds(r * share, share)] - step_master * total
    value = smooth_packed(updated).astype(jnp.bfloat16)
    fresh[...] = value
    table_ref[pl.ds(mine, share)] = value

    def end_part(t, carry):
        part_copy(t).wait_send()
        return carry

    lax.fori_loop(1, count, end_part, 0)

    gather_levels(n_row, n_col, fresh, table_ref, stored, send2_sem, recv2_sem)


def update_masters(sums, own, n_row, n_col):
    count = n_row * n_col
    piece = (own.shape[0] // n_row,) + own.shape[1:]
    return pl.pallas_call(
        functools.partial(update_kernel, n_row, n_col),
        in_specs=[VM, VM],
        out_specs=VM,
        out_shape=jax.ShapeDtypeStruct(sums.shape, jnp.bfloat16),
        scratch_shapes=[
            pltpu.VMEM((count,) + piece, jnp.bfloat16),
            pltpu.VMEM(piece, jnp.bfloat16),
            pltpu.SemaphoreType.DMA((count,)),
            pltpu.SemaphoreType.DMA((count,)),
            *gather_sems(n_row, n_col),
        ],
        compiler_params=pltpu.CompilerParams(collective_id=2, has_side_effects=True),
        name="update_masters",
    )(sums, own)


def per_device(
    masters, inst_master, inst_orient, owner_map, tile_free, target, kernel_spectra, socs_weights
):
    stored = masters.shape[0]
    total = owner_map.shape[0]
    consts = tables(TILE + 2 * HALO, kernel_spectra.shape[1], HALO, TILE)
    rows_place, rows_t, cols_place = placements()
    own = masters.reshape(stored, HALF, LANES)
    n_row = lax.axis_size("row")
    n_col = lax.axis_size("col")
    table = gather_masters(own.astype(jnp.bfloat16), n_row, n_col)
    shading, mask, edge_l, edge_r = image(
        inst_master, inst_orient, owner_map, table, tile_free, rows_place, cols_place, True
    )
    padded = with_halo(mask, edge_l, edge_r, n_row, n_col)
    resist, new_free, sums = tile_steps(
        inst_master, inst_orient, owner_map, socs_weights, padded, target, shading, tile_free,
        kernel_spectra, consts, rows_t, cols_place, total,
    )
    table = update_masters(sums, own, n_row, n_col)
    fresh = lax.dynamic_slice_in_dim(table, lax.axis_index("col") * stored, stored, 0)
    (new_mask,) = image(
        inst_master, inst_orient, owner_map, table, new_free, rows_place, cols_place, False
    )
    return (resist, new_mask, fresh.astype(jnp.float32).reshape(masters.shape))


def solution(mesh):
    in_specs = (
        P("col", None),
        P("row", "col"),
        P("row", "col"),
        P(),
        P("row", "col"),
        P("row", "col"),
        P(),
        P(),
    )
    out_specs = (P("row", "col"), P("row", "col"), P("col", None))
    return jax.shard_map(
        per_device, mesh=mesh, in_specs=in_specs, out_specs=out_specs, check_vma=False
    )
```
